256 devices in a mesh: dst: 32 (over y, z), src: 8 (over x, core).
Axes of the slice: x: 4, y: 4, z: 8, core: 2. Of those that a mesh axis runs over, the one named last changes fastest.
Arguments:
- transitions: bfloat16 [16384, 128, 128], P(('dst', 'src')), may hold values from 0.0009994507 to 1
- row_block: int32 [16384], P(('dst', 'src')), may hold values from -1 to 1023, as said below
- col_block: int32 [16384], P(('dst', 'src')), may hold values from -1 to 1023, as said below
- beta_last: float32 [32, 128, 8, 128], P(None, 'dst', 'src'), may hold values from 0.2 to 2
- emissions: bfloat16 [2, 32, 128, 8, 128], P(None, None, 'dst', 'src'), may hold values from 0.019897461 to 1
- forward: bfloat16 [2, 32, 128, 8, 128], P(None, None, 'dst', 'src'), may hold values from 0.03 to 125, as said below
Outputs:
- counts: bfloat16 [16384, 128, 128], P(('dst', 'src'))
- beta_first: float32 [32, 128, 8, 128], P(None, 'dst', 'src')
- log_norms: float32 [2, 32], replicated
The draws below stay inside these ranges and needn't reach their ends.
Inputs may be any that keep to these rules, and one draw needn't show every extreme that they name: `row_block`: slots are grouped by device (index dst * 8 + src), 64 to a device. A live slot holds a block whose source block number r has r % 8 equal to the device's src index and whose destination block lies in the device's dst index's own consecutive equal share of blocks; no block appears twice; live slots come first, and empty ones hold -1 in both arrays. One device has all 64 slots live; each device has at least one. `col_block`: same slots as row_block; -1 exactly where row_block is -1. `forward`: Positive.
All inputs are finite; a program needn't handle non-finite values.
Results may differ from the reference program's by a relative error of at most 0.0029.
Values may be sent and summed in bfloat16 or wider, within the bound.
No kernel may reach another device: no remote copies, remote signals or barrier semaphores. Data moves between devices by JAX's collectives and lax.ppermute only.
A program may use at most 64 MiB of HBM per device.

```python
import math
import jax
import jax.numpy as jnp
from jax import lax

S = 131072
BLK = 128
B = 32
CAP = 64
STEPS = 2
ROW_SPAN = 128
SLOTS = 16384
N_DST = 32
N_SRC = 8


def pick_slots(sub_key, candidates):
    return jax.random.permutation(sub_key, candidates)[:CAP].astype(jnp.int32)


def pattern(key):
    tile_total = N_DST * N_SRC
    row_span = S // (BLK * N_SRC)
    col_span = S // (BLK * N_DST)
    key_count, key_busy, key_perm = jax.random.split(jax.random.fold_in(key, 7), 3)
    filled = jax.random.randint(key_count, (tile_total,), 1, CAP + 1).astype(jnp.int32)
    busiest = jax.random.randint(key_busy, (), 0, tile_total).astype(jnp.int32)
    tile_ids = jnp.arange(tile_total, dtype=jnp.int32)
    filled = jnp.where(tile_ids == busiest, CAP, filled)
    sub_keys = jax.random.split(key_perm, tile_total)
    chosen = jax.vmap(lambda sub_key: pick_slots(sub_key, row_span * col_span))(sub_keys)
    row_ids = chosen // col_span * N_SRC + (tile_ids % N_SRC)[:, None]
    col_ids = (tile_ids // N_SRC)[:, None] * col_span + chosen % col_span
    living = jnp.arange(CAP, dtype=jnp.int32)[None, :] < filled[:, None]
    row_out = jnp.where(living, row_ids, -1).reshape(-1).astype(jnp.int32)
    col_out = jnp.where(living, col_ids, -1).reshape(-1).astype(jnp.int32)
    return (row_out, col_out)


def draw_row_block(key, part):
    return pattern(key)[0]


def draw_col_block(key, part):
    return pattern(key)[1]


def draw_forward(key, part):
    row_span = S // (BLK * N_SRC)
    key_state, key_seq, key_rough = jax.random.split(jax.random.fold_in(key, 11), 3)
    position = jnp.arange(S, dtype=jnp.float32).reshape(1, 1, row_span, N_SRC, BLK)
    ramped = 1.0 + 2.0 * position / S
    state_scale = jnp.exp(jax.random.uniform(key_state, (1, 1, row_span, N_SRC, BLK), jnp.float32, 0.0, math.log(10.0)))
    seq_scale = jnp.exp(jax.random.uniform(key_seq, (1, B, 1, 1, 1), jnp.float32, 0.0, math.log(10.0)))
    rough = jnp.exp(jax.random.uniform(key_rough, (STEPS, B, row_span, N_SRC, BLK), jnp.float32, -0.9, 0.9))
    return (0.1 * ramped * state_scale * seq_scale * rough).astype(jnp.bfloat16)


def levels(own_key, dims, cuts, smallest, top_value):
    loudness, own = 1.0, jax.random.fold_in(own_key, 6)
    for dim, blocks in cuts:
        heights = jnp.exp(jax.random.uniform(jax.random.fold_in(own, dim), (blocks,), jnp.float32, smallest / len(cuts), top_value / len(cuts)))
        loudness = loudness * jnp.repeat(heights, dims[dim] // blocks).reshape([-1 if axis == dim else 1 for axis in range(len(dims))])
    return loudness


def setup_inputs(seed: int = 0) -> dict:
    keys = jax.random.split(jax.random.key(seed), 7)
    return {
        "transitions": jnp.clip(jnp.exp(math.log(1.0) - 6.9083047 * jax.random.uniform(keys[0], (SLOTS, BLK, BLK), jnp.float32) ** levels(keys[0], (SLOTS, BLK, BLK), ((0, 256),), -0.2, 0.2)), 0.0009994507, 1.0).astype(jnp.bfloat16),
        "row_block": draw_row_block(jax.random.fold_in(keys[6], 71), 0),
        "col_block": draw_col_block(jax.random.fold_in(keys[6], 71), 0),
        "beta_last": jnp.clip(jnp.exp(math.log(2.0) - 2.3025851 * jax.random.uniform(keys[3], (B, ROW_SPAN, N_SRC, BLK), jnp.float32) ** levels(keys[3], (B, ROW_SPAN, N_SRC, BLK), ((1, 32), (2, 8)), -0.2, 0.2)), 0.2, 2.0),
        "emissions": jnp.clip(jnp.exp(math.log(1.0) - 3.9171631 * jax.random.uniform(keys[4], (STEPS, B, ROW_SPAN, N_SRC, BLK), jnp.float32) ** levels(keys[4], (STEPS, B, ROW_SPAN, N_SRC, BLK), ((2, 32), (3, 8)), -0.2, 0.2)), 0.019897461, 1.0).astype(jnp.bfloat16),
        "forward": draw_forward(jax.random.fold_in(keys[6], 71), 0),
    }


def reference(transitions, row_block, col_block, beta_last, emissions, forward):
    tile_total = N_DST * N_SRC
    slot_blocks = transitions.reshape(tile_total, CAP, BLK, BLK)
    rows_all = row_block.reshape(tile_total, CAP)
    cols_all = col_block.reshape(tile_total, CAP)
    total_blocks = S // BLK
    seq_count = beta_last.shape[0]
    beta_now = beta_last.reshape(seq_count, total_blocks, BLK)
    alpha_list = []
    scaled_list = []
    log_list = []
    for step_index in range(STEPS):
        emitted = emissions[step_index].reshape(seq_count, total_blocks, BLK)
        message = (emitted.astype(jnp.float32) * beta_now).astype(jnp.bfloat16)
        message_blocks = jnp.transpose(message, (1, 0, 2))

        def one_tile(running, tile_data):
            trans_tile, rows_tile, cols_tile = tile_data
            living = rows_tile >= 0
            cols_safe = jnp.where(living, cols_tile, 0).astype(jnp.int32)
            rows_safe = jnp.where(living, rows_tile, 0).astype(jnp.int32)
            picked = message_blocks[cols_safe].astype(jnp.float32)
            products = jnp.einsum("cbj,cij->cbi", picked, trans_tile.astype(jnp.float32))
            products = products * living.astype(jnp.float32)[:, None, None]
            return running.at[rows_safe].add(products), None

        start = jnp.zeros((total_blocks, seq_count, BLK), jnp.float32)
        raw_sums = lax.scan(one_tile, start, (slot_blocks, rows_all, cols_all))[0]
        alpha_blocks = jnp.transpose(forward[step_index].reshape(seq_count, total_blocks, BLK), (1, 0, 2))
        scale_now = jnp.sum(alpha_blocks.astype(jnp.float32) * raw_sums, axis=(0, 2)) / S
        beta_now = jnp.transpose(raw_sums / scale_now[None, :, None], (1, 0, 2))
        scaled = (message_blocks.astype(jnp.float32) / scale_now[None, :, None]).astype(jnp.bfloat16)
        alpha_list.append(alpha_blocks)
        scaled_list.append(scaled)
        log_list.append(jnp.log(scale_now))
    alpha_stack = jnp.stack(alpha_list)
    scaled_stack = jnp.stack(scaled_list)

    def tile_counts(tile_data):
        trans_tile, rows_tile, cols_tile = tile_data
        living = rows_tile >= 0
        cols_safe = jnp.where(living, cols_tile, 0).astype(jnp.int32)
        rows_safe = jnp.where(living, rows_tile, 0).astype(jnp.int32)
        alpha_picked = alpha_stack[:, rows_safe].astype(jnp.float32)
        scaled_picked = scaled_stack[:, cols_safe].astype(jnp.float32)
        count_sum = jnp.einsum("tcbi,tcbj->cij", alpha_picked, scaled_picked)
        masked = count_sum * trans_tile.astype(jnp.float32) * living.astype(jnp.float32)[:, None, None]
        return masked.astype(jnp.bfloat16)

    counts = lax.map(tile_counts, (slot_blocks, rows_all, cols_all)).reshape(tile_total * CAP, BLK, BLK)
    beta_first = beta_now.reshape(seq_count, total_blocks // N_SRC, N_SRC, BLK)
    return counts, beta_first, jnp.stack(log_list)
```

```python
import functools

import jax
import jax.numpy as jnp
from jax import lax
from jax.experimental import pallas as pl
from jax.experimental.pallas import tpu as pltpu
from jax.sharding import Mesh
from jax.sharding import PartitionSpec as P

S = 131072
STEPS = 2
NY, NZ, NX, NC = 4, 8, 4, 2
DST = ("y", "z")
SRC = ("x", "c")
ALL = DST + SRC
F32 = jnp.float32
BF16 = jnp.bfloat16
LIMIT = 24 * 1024 * 1024


def vmem(count):
    return [pl.BlockSpec(memory_space=pltpu.VMEM)] * count


def smem(count):
    return [pl.BlockSpec(memory_space=pltpu.SMEM)] * count


def row_of(column, offset):
    b = column.shape[0]
    lane = lax.broadcasted_iota(jnp.int32, (b, 128), 1)
    seq = lax.broadcasted_iota(jnp.int32, (b, 128), 0)
    return jnp.sum(jnp.where(lane == seq + offset, column, 0.0), axis=0, keepdims=True)


def column_of(row, offset, b):
    lane = lax.broadcasted_iota(jnp.int32, (b, 128), 1)
    seq = lax.broadcasted_iota(jnp.int32, (b, 128), 0)
    wide = jnp.broadcast_to(row, (b, 128))
    return jnp.sum(jnp.where(lane == seq + offset, wide, 0.0), axis=1, keepdims=True)


def multiply_slots(index, pieces, blocks, cols, acc):
    rows = pieces[0].shape[0]
    for n, piece in enumerate(pieces):
        cols[n * rows : (n + 1) * rows] = piece[...]
    acc[...] = jnp.zeros_like(acc)
    group = 8

    def several(g, carry):
        for n in range(group):
            m = g * group + n
            product = lax.dot_general(
                cols[index[1, m]],
                blocks[m],
                (((1,), (1,)), ((), ())),
                preferred_element_type=F32,
            )
            row = index[0, m]
            acc[row] = acc[row] + product
        return carry

    lax.fori_loop(0, blocks.shape[0] // group, several, 0)


def first_step(index, *refs):
    pieces, (blocks, out, cols, acc) = refs[:8], refs[8:]
    multiply_slots(index, pieces, blocks, cols, acc)
    total = out.shape[0] * out.shape[1]
    out[...] = acc[:total].astype(BF16).reshape(out.shape)


def second_step(index, place, *refs):
    pieces, forwards, (blocks, first_sum, out, norms, cols, acc) = refs[:8], refs[8:12], refs[12:]
    multiply_slots(index, pieces, blocks, cols, acc)
    total = out.shape[0] * out.shape[1]
    out[...] = acc[:total].astype(BF16).reshape(out.shape)
    b = out.shape[2]
    rows = forwards[0].shape[0]
    y = place[0]
    value = jnp.zeros((b, 128), F32)
    for k, alpha in enumerate(forwards):
        base = lax.rem(y - k + NY, NY) * rows
        for r in range(rows):
            value = value + acc[base + r] * alpha[r, 1].astype(F32)
    part = row_of(jnp.sum(value, axis=1, keepdims=True), b)
    both = part + first_sum[...]
    norms[...] = jnp.broadcast_to(both[None], norms.shape)


def reduce_first(received, emitted, alpha, message, norm):
    total = received[0].astype(F32)
    for d in range(1, received.shape[0]):
        total = total + received[d].astype(F32)
    message[...] = (emitted[...].astype(F32) * total).astype(BF16)
    value = jnp.sum(total * alpha[...].astype(F32), axis=0)
    norm[...] = row_of(jnp.sum(value, axis=1, keepdims=True), 0)


def reduce_last(received, norms, out):
    total = received[0].astype(F32)
    for d in range(1, received.shape[0]):
        total = total + received[d].astype(F32)
    b = total.shape[1]
    norm = jnp.sum(norms[...], axis=0)
    inverse = S / column_of(norm, b, b)
    for a in range(total.shape[0]):
        out[:, a, :] = total[a] * inverse


def count_slots(index, live, *refs):
    pieces, forwards, (norms, blocks, out, logs, weighted, alphas) = refs[:16], refs[16:20], refs[20:]
    rows, b = pieces[0].shape[0], pieces[0].shape[1]

    @pl.when(pl.program_id(0) == 0)
    def _():
        norm = jnp.sum(norms[...], axis=0)
        for k in range(STEPS):
            column = column_of(norm, k * b, b)
            inverse = S / column
            for n in range(8):
                piece = pieces[8 * k + n][...].astype(F32)
                weighted[n * rows : (n + 1) * rows, k] = (piece * inverse).astype(BF16)
        per = forwards[0].shape[0]
        for k, alpha in enumerate(forwards):
            alphas[k * per : (k + 1) * per] = alpha[...]
        lane = lax.broadcasted_iota(jnp.int32, (1, 128), 1)
        first = jnp.where(lane < b, norm, 1.0)
        second = jnp.where((lane >= b) & (lane < 2 * b), norm, 1.0)
        moved = pltpu.roll(second, 128 - b, 1)
        logs[0:1, :] = jnp.log(first / S)
        logs[1:2, :] = jnp.log(moved / first)

    step = pl.program_id(0)
    for n in range(out.shape[0]):
        m = step * out.shape[0] + n
        left = alphas[index[2, m]].reshape(STEPS * b, 128)
        right = weighted[index[1, m]].reshape(STEPS * b, 128)
        total = lax.dot_general(
            left, right, (((0,), (0,)), ((), ())), preferred_element_type=F32
        )
        value = total * blocks[n].astype(F32)
        out[n] = jnp.where(m < live[0], value, 0.0).astype(BF16)


def gather_src(piece):
    found = [piece]
    for k in range(1, NX):
        found.append(lax.ppermute(piece, "x", [(i, (i + k) % NX) for i in range(NX)]))
    out = []
    for item in found:
        out.append(item)
        out.append(lax.ppermute(item, "c", [(0, 1), (1, 0)]))
    return out


def body(transitions, row_block, col_block, beta_last, emissions, forward):
    slots = transitions.shape[0]
    b, rows, width = beta_last.shape[0], beta_last.shape[1], beta_last.shape[3]
    owners = NY * NZ
    src = NX * NC
    total_rows = rows * owners
    y, x, c = lax.axis_index("y"), lax.axis_index("x"), lax.axis_index("c")

    living = row_block >= 0
    row_local = jnp.where(living, row_block // src, 0)
    col_local = jnp.where(living, col_block % (rows * src), 0)
    col_src = col_local % src
    place = ((x - col_src // NC) % NX) * NC + (col_src % NC + c) % NC
    col_index = place * rows + col_local // src
    per = total_rows // NY
    alpha_index = ((y - row_local // per) % NY) * per + row_local % per
    index = jnp.stack([jnp.where(living, row_local, total_rows), col_index, alpha_index])
    live = jnp.sum(living.astype(jnp.int32)).reshape(1)
    y_place = y.astype(jnp.int32).reshape(1)

    emitted = jnp.transpose(emissions[:, :, :, 0, :], (0, 2, 1, 3))
    alpha = jnp.transpose(forward[:, :, :, 0, :], (2, 0, 1, 3))
    beta = jnp.transpose(beta_last[:, :, 0, :], (1, 0, 2))
    message = (emitted[0].astype(F32) * beta).astype(BF16)

    pieces = gather_src(message)

    spread = jnp.broadcast_to(alpha[None], (NZ,) + alpha.shape)
    column = lax.all_to_all(spread, "z", 0, 0)
    column = column.reshape((NZ * rows,) + alpha.shape[1:])
    forwards = [column] + [
        lax.ppermute(column, "y", [(i, (i + k) % NY) for i in range(NY)]) for k in range(1, NY)
    ]

    partial_shape = jax.ShapeDtypeStruct((owners, rows, b, width), BF16)
    slot_scratch = [
        pltpu.VMEM((src * rows, b, width), BF16),
        pltpu.VMEM((total_rows + 8, b, width), F32),
    ]
    params = pltpu.CompilerParams(vmem_limit_bytes=LIMIT)

    sent = pl.pallas_call(
        first_step,
        out_shape=partial_shape,
        in_specs=smem(1) + vmem(9),
        out_specs=vmem(1)[0],
        scratch_shapes=slot_scratch,
        compiler_params=params,
        name="first_step",
    )(index, *pieces, transitions)
    received = lax.all_to_all(sent, DST, 0, 0)

    message_1, norm_0 = pl.pallas_call(
        reduce_first,
        out_shape=(
            jax.ShapeDtypeStruct((rows, b, width), BF16),
            jax.ShapeDtypeStruct((1, 128), F32),
        ),
        in_specs=vmem(3),
        out_specs=tuple(vmem(2)),
        compiler_params=params,
        name="reduce_first",
    )(received, emitted[1], alpha[:, 0])
    pieces_1 = gather_src(message_1)

    sent_1, norms = pl.pallas_call(
        second_step,
        out_shape=(partial_shape, jax.ShapeDtypeStruct((owners * src, 1, 128), F32)),
        in_specs=smem(2) + vmem(14),
        out_specs=tuple(vmem(2)),
        scratch_shapes=slot_scratch,
        compiler_params=params,
        name="second_step",
    )(index, y_place, *pieces_1, *forwards, transitions, norm_0)
    received_1 = lax.all_to_all(sent_1, DST, 0, 0)
    all_norms = lax.all_to_all(norms, ALL, 0, 0)

    group = 8
    whole = lambda shape: pl.BlockSpec(shape, lambda i: (0,) * len(shape))
    part = pl.BlockSpec((group, width, width), lambda i: (i, 0, 0))
    counts, logs = pl.pallas_call(
        count_slots,
        grid=(slots // group,),
        out_shape=(
            jax.ShapeDtypeStruct((slots, width, width), BF16),
            jax.ShapeDtypeStruct((STEPS, 128), F32),
        ),
        in_specs=smem(2)
        + [whole((rows, b, width))] * 16
        + [whole((NZ * rows, STEPS, b, width))] * 4
        + [whole((owners * src, 1, 128)), part],
        out_specs=(part, whole((STEPS, 128))),
        scratch_shapes=[
            pltpu.VMEM((src * rows, STEPS, b, width), BF16),
            pltpu.VMEM((total_rows, STEPS, b, width), BF16),
        ],
        compiler_params=params,
        name="count_slots",
    )(index, live, *pieces, *pieces_1, *forwards, all_norms, transitions)

    beta_first = pl.pallas_call(
        reduce_last,
        out_shape=jax.ShapeDtypeStruct((b, rows, width), F32),
        in_specs=vmem(2),
        out_specs=vmem(1)[0],
        compiler_params=params,
        name="reduce_last",
    )(received_1, all_norms)
    return counts, beta_first[:, :, None, :], logs[:, :b]


def solution(mesh):
    fine = Mesh(mesh.devices.reshape(NY, NZ, NX, NC), ALL)
    return jax.shard_map(
        body,
        mesh=fine,
        in_specs=(
            P(ALL, None, None),
            P(ALL),
            P(ALL),
            P(None, DST, SRC, None),
            P(None, None, DST, SRC, None),
            P(None, None, DST, SRC, None),
        ),
        out_specs=(P(ALL, None, None), P(None, DST, SRC, None), P()),
        check_vma=False,
    )
```

```python
import jax
import jax.numpy as jnp
from jax import lax
from jax.experimental import pallas as pl
from jax.experimental.pallas import tpu as pltpu
from jax.sharding import Mesh
from jax.sharding import PartitionSpec as P


S = 131072
STEPS = 2
NY, NH, NL, NX, NC = 4, 4, 2, 4, 2
NZ = NH * NL
SRC_COUNT = NX * NC
DST = ("y", "zh", "zl")
SRC = ("x", "c")
ALL = DST + SRC
F32 = jnp.float32
BF16 = jnp.bfloat16
GRANT = 60 * 1024
EXTRA = 8
CHUNKS = 8
COUNT_GROUP = 16
GROUP = 8


def room(kib):
    return pltpu.CompilerParams(vmem_limit_bytes=(GRANT - kib) * 1024)


def vmem(count):
    return [pl.BlockSpec(memory_space=pltpu.VMEM)] * count


def hbm(count):
    return [pl.BlockSpec(memory_space=pltpu.HBM)] * count


def smem(count):
    return [pl.BlockSpec(memory_space=pltpu.SMEM)] * count


def row_of(column, offset):
    b = column.shape[0]
    lane = lax.broadcasted_iota(jnp.int32, (b, 128), 1)
    seq = lax.broadcasted_iota(jnp.int32, (b, 128), 0)
    return jnp.sum(jnp.where(lane == seq + offset, column, 0.0), axis=0, keepdims=True)


def column_of(row, offset, b):
    lane = lax.broadcasted_iota(jnp.int32, (b, 128), 1)
    seq = lax.broadcasted_iota(jnp.int32, (b, 128), 0)
    wide = jnp.broadcast_to(row, (b, 128))
    return jnp.sum(jnp.where(lane == seq + offset, wide, 0.0), axis=1, keepdims=True)


def tree(values):
    while len(values) > 1:
        values = [values[n] + values[n + 1] for n in range(0, len(values), 2)]
    return values[0]


def over_slots(first, count, step):
    def several(g, carry):
        for n in range(GROUP):
            step(first + g * GROUP + n)
        return carry

    lax.fori_loop(0, count // GROUP, several, 0)


def load_blocks(blocks, held, sems):
    size = held.shape[0] // CHUNKS
    copies = []
    for n in range(CHUNKS):
        part = pl.ds(n * size, size)
        copies.append(pltpu.make_async_copy(blocks.at[part], held.at[part], sems.at[n]))
        copies[-1].start()
    return copies


def over_chunks(copies, held, step):
    size = held.shape[0] // CHUNKS
    for n, copy in enumerate(copies):
        copy.wait()
        over_slots(n * size, size, step)


def split_three(value, rows):
    high = value.astype(BF16).astype(F32)
    middle = (value - high).astype(BF16).astype(F32)
    low = value - high - middle
    line = lax.broadcasted_iota(jnp.int32, (rows, 128), 0)
    return jnp.where(
        line == 0, high, jnp.where(line == 1, middle, jnp.where(line == 2, low, 0.0))
    )


def multiply_slots(index, copies, held, cols, acc):
    acc[...] = jnp.zeros_like(acc)

    def step(m):
        product = lax.dot_general(
            cols[index[1, m]],
            held[m],
            (((1,), (1,)), ((), ())),
            preferred_element_type=F32,
        )
        row = index[0, m]
        acc[row] = acc[row] + product

    over_chunks(copies, held, step)


def send_partials(acc, ready, out, sems, extra=None):
    owners, lines = ready.shape[0], ready.shape[1]
    rows = acc.shape[0] // owners
    kept = rows * acc.shape[1]
    size = owners // CHUNKS
    copies = []
    for n in range(CHUNKS):
        part = pl.ds(n * size, size)
        value = acc[n * size * rows : (n + 1) * size * rows].astype(BF16)
        ready[part, :kept] = value.reshape(size, kept, 128)
        if extra is not None:
            ready[part, kept:] = jnp.broadcast_to(extra[None], (size, lines - kept, 128))
        copies.append(pltpu.make_async_copy(ready.at[part], out.at[part], sems.at[n]))
        copies[-1].start()
    return copies


def first_step(index, *refs):
    pieces, (blocks, out, cols_out) = refs[:SRC_COUNT], refs[SRC_COUNT : SRC_COUNT + 3]
    cols, acc, held, ready, in_sems, out_sems, col_sem = refs[SRC_COUNT + 3 :]
    copies = load_blocks(blocks, held, in_sems)
    rows = pieces[0].shape[0]
    for n, piece in enumerate(pieces):
        cols[n * rows : (n + 1) * rows] = piece[...]
    keep = pltpu.make_async_copy(cols, cols_out, col_sem)
    keep.start()
    multiply_slots(index, copies, held, cols, acc)
    for copy in send_partials(acc, ready, out, out_sems):
        copy.wait()
    keep.wait()


def second_step(index, *refs):
    pieces, (blocks, out, cols_out) = refs[:SRC_COUNT], refs[SRC_COUNT : SRC_COUNT + 3]
    cols, acc, held, ready, in_sems, out_sems, col_sem = refs[SRC_COUNT + 3 :]
    copies = load_blocks(blocks, held, in_sems)
    b = acc.shape[1]
    rows = cols.shape[0] // SRC_COUNT
    parts = []
    for n, piece in enumerate(pieces):
        cols[n * rows : (n + 1) * rows] = piece[: rows * b].reshape(rows, b, 128)
        parts.append(jnp.sum(piece[rows * b :].astype(F32), axis=0, keepdims=True))
    keep = pltpu.make_async_copy(cols, cols_out, col_sem)
    keep.start()
    extra = split_three(tree(parts), EXTRA).astype(BF16)
    multiply_slots(index, copies, held, cols, acc)
    for copy in send_partials(acc, ready, out, out_sems, extra):
        copy.wait()
    keep.wait()


def back_products(index, *refs):
    forwards, (blocks, *outs) = refs[:NY], refs[NY : NY + 1 + SRC_COUNT]
    alphas, acc, held, in_sems, alpha_sems = refs[NY + 1 + SRC_COUNT :]
    per = forwards[0].shape[0]
    loads = []
    for n, alpha in enumerate(forwards):
        part = pl.ds(n * per, per)
        loads.append(pltpu.make_async_copy(alpha, alphas.at[part], alpha_sems.at[n]))
        loads[-1].start()
    copies = load_blocks(blocks, held, in_sems)
    acc[...] = jnp.zeros_like(acc)
    for load in loads:
        load.wait()

    def step(m):
        product = jnp.dot(alphas[index[2, m]], held[m], preferred_element_type=F32)
        col = index[3, m]
        acc[col] = acc[col] + product

    over_chunks(copies, held, step)
    rows = outs[0].shape[0]
    for n, out in enumerate(outs):
        out[...] = acc[n * rows : (n + 1) * rows].astype(BF16)


def add_received(received):
    total = received[0].astype(F32)
    for d in range(1, received.shape[0]):
        total = total + received[d].astype(F32)
    return total


def reduce_first(received, emitted, alpha, *refs):
    backs, message = refs[:SRC_COUNT], refs[SRC_COUNT]
    rows, b = emitted.shape[0], emitted.shape[1]
    total = add_received(received).reshape(rows, b, 128)
    sent = (emitted[...].astype(F32) * total).astype(BF16)
    message[: rows * b] = sent.reshape(rows * b, 128)
    back = tree([piece[...].astype(F32) for piece in backs])
    first = jnp.sum(total * alpha[...].astype(F32), axis=0)
    second = jnp.sum(sent.astype(F32) * back, axis=0)
    norm = row_of(jnp.sum(first, axis=1, keepdims=True), 0)
    norm = norm + row_of(jnp.sum(second, axis=1, keepdims=True), b)
    message[rows * b :] = split_three(norm, EXTRA).astype(BF16)


def norm_of(lines):
    return jnp.sum(jnp.sum(lines.astype(F32), axis=0), axis=0, keepdims=True)


def slot_rows(index, *refs):
    forwards, (out, alphas, sems) = refs[: STEPS * NY], refs[STEPS * NY :]
    per = forwards[0].shape[0]

    @pl.when(pl.program_id(0) == 0)
    def _():
        copies = []
        for k in range(STEPS):
            for n in range(NY):
                at = NY * k + n
                target = alphas.at[pl.ds(n * per, per), k]
                copies.append(pltpu.make_async_copy(forwards[at], target, sems.at[at]))
                copies[-1].start()
        for copy in copies:
            copy.wait()

    step = pl.program_id(0)
    for n in range(out.shape[0]):
        m = step * out.shape[0] + n
        out[n] = alphas[index[2, m]].reshape(out.shape[2], 128).T


def count_slots(index, *refs):
    messages = refs[:STEPS]
    received, left, blocks, out, beta, logs = refs[STEPS : STEPS + 6]
    held, lines, weighted, sems, line_sem = refs[STEPS + 6 :]
    b = weighted.shape[2]
    cols = held.shape[1]

    @pl.when(pl.program_id(0) == 0)
    def _():
        kept = received.shape[1] - EXTRA
        copies = [pltpu.make_async_copy(received, lines, line_sem)]
        for k in range(STEPS):
            copies.append(pltpu.make_async_copy(messages[k], held.at[k], sems.at[k]))
        for copy in copies:
            copy.start()
        for copy in copies:
            copy.wait()
        norm = norm_of(lines[:, kept:])
        weighted[cols] = jnp.zeros((STEPS, b, 128), BF16)
        for k in range(STEPS):
            inverse = S / column_of(norm, k * b, b)
            weighted[:cols, k] = (held[k].astype(F32) * inverse).astype(BF16)
        total = lines[0, :kept].astype(F32)
        for d in range(1, lines.shape[0]):
            total = total + lines[d, :kept].astype(F32)
        inverse = S / column_of(norm, b, b)
        for a in range(kept // b):
            beta[:, a, :] = total[a * b : (a + 1) * b] * inverse
        lane = lax.broadcasted_iota(jnp.int32, (1, 128), 1)
        first = jnp.where(lane < b, norm, 1.0)
        second = jnp.where((lane >= b) & (lane < 2 * b), norm, 1.0)
        moved = pltpu.roll(second, 128 - b, 1)
        logs[0:1, :] = jnp.log(first / S)
        logs[1:2, :] = jnp.log(moved / first)

    step = pl.program_id(0)
    for n in range(out.shape[0]):
        m = step * out.shape[0] + n
        right = weighted[index[3, m]].reshape(STEPS * b, 128)
        total = jnp.dot(left[n], right, preferred_element_type=F32)
        out[n] = (total * blocks[n].astype(F32)).astype(BF16)


def across(value, axis, size, k):
    return lax.ppermute(value, axis, [(i, i ^ k) for i in range(size)])


def gather_src(piece):
    found = [piece] + [across(piece, "x", NX, k) for k in range(1, NX)]
    out = []
    for item in found:
        out.append(item)
        out.append(across(item, "c", NC, 1))
    return out


def gather_y(column):
    return [column] + [across(column, "y", NY, k) for k in range(1, NY)]


def steps(transitions, row_block, col_block, beta_last, emissions, forward):
    slots = transitions.shape[0]
    b, rows, width = beta_last.shape[0], beta_last.shape[1], beta_last.shape[3]
    owners = NY * NZ
    total_rows = rows * owners
    total_cols = rows * SRC_COUNT
    y = lax.axis_index("y")
    mine = lax.axis_index(SRC)

    living = row_block >= 0
    row_local = jnp.where(living, row_block // SRC_COUNT, 0)
    col_local = jnp.where(living, col_block % total_cols, 0)
    col_index = ((col_local % SRC_COUNT) ^ mine) * rows + col_local // SRC_COUNT
    per = total_rows // NY
    alpha_index = ((row_local // per) ^ y) * per + row_local % per
    index = jnp.stack(
        [
            jnp.where(living, row_local, total_rows),
            col_index,
            alpha_index,
            jnp.where(living, col_index, total_cols),
        ]
    )

    emitted = jnp.transpose(emissions[:, :, :, 0, :], (0, 2, 1, 3))
    alpha = jnp.transpose(forward[:, :, :, 0, :], (0, 2, 1, 3))
    beta = jnp.transpose(beta_last[:, :, 0, :], (1, 0, 2))
    message = (emitted[0].astype(F32) * beta).astype(BF16)
    spread = jnp.broadcast_to(alpha[:, None], (STEPS, NZ) + alpha.shape[1:])
    piece_shape = jax.ShapeDtypeStruct((rows, b, width), BF16)

    pieces = gather_src(message)

    columns = lax.all_to_all(spread, ("zh", "zl"), 1, 1)
    columns = columns.reshape(STEPS, NZ * rows, b, width)
    forwards_1 = gather_y(columns[1])
    forwards_0 = gather_y(columns[0])

    def partial_shape(lines):
        return jax.ShapeDtypeStruct((owners, lines, width), BF16)

    def slot_scratch(lines):
        return [
            pltpu.VMEM((total_cols, b, width), BF16),
            pltpu.VMEM((total_rows + 8, b, width), F32),
            pltpu.VMEM((slots, width, width), BF16),
            pltpu.VMEM((owners, lines, width), BF16),
            pltpu.SemaphoreType.DMA((CHUNKS,)),
            pltpu.SemaphoreType.DMA((CHUNKS,)),
            pltpu.SemaphoreType.DMA,
        ]

    lines = rows * b
    cols_shape = jax.ShapeDtypeStruct((total_cols, b, width), BF16)

    sent, cols_0 = pl.pallas_call(
        first_step,
        out_shape=(partial_shape(lines), cols_shape),
        in_specs=smem(1) + vmem(SRC_COUNT) + hbm(1),
        out_specs=tuple(hbm(2)),
        scratch_shapes=slot_scratch(lines),
        compiler_params=room(9000),
        name="first_step",
    )(index, *pieces, transitions)
    received = lax.all_to_all(sent, DST, 0, 0)

    backs = pl.pallas_call(
        back_products,
        out_shape=(piece_shape,) * SRC_COUNT,
        in_specs=smem(1) + hbm(NY + 1),
        out_specs=tuple(vmem(SRC_COUNT)),
        scratch_shapes=[
            pltpu.VMEM((total_rows, b, width), BF16),
            pltpu.VMEM((total_cols + 8, b, width), F32),
            pltpu.VMEM((slots, width, width), BF16),
            pltpu.SemaphoreType.DMA((CHUNKS,)),
            pltpu.SemaphoreType.DMA((NY,)),
        ],
        compiler_params=room(9000),
        name="back_products",
    )(index, *forwards_1, transitions)
    backs = [backs[0]] + [across(backs[n], SRC, SRC_COUNT, n) for n in range(1, SRC_COUNT)]

    message_1 = pl.pallas_call(
        reduce_first,
        out_shape=jax.ShapeDtypeStruct((lines + EXTRA, width), BF16),
        in_specs=vmem(3 + SRC_COUNT),
        out_specs=vmem(1)[0],
        compiler_params=room(9000),
        name="reduce_first",
    )(received, emitted[1], alpha[0], *backs)
    pieces_1 = gather_src(message_1)

    sent_1, cols_1 = pl.pallas_call(
        second_step,
        out_shape=(partial_shape(lines + EXTRA), cols_shape),
        in_specs=smem(1) + vmem(SRC_COUNT) + hbm(1),
        out_specs=tuple(hbm(2)),
        scratch_shapes=slot_scratch(lines + EXTRA),
        compiler_params=room(9000),
        name="second_step",
    )(index, *pieces_1, transitions)
    received_1 = lax.all_to_all(sent_1, DST, 0, 0)

    part = pl.BlockSpec((COUNT_GROUP, width, width), lambda i: (i, 0, 0))
    left_part = pl.BlockSpec((COUNT_GROUP, width, STEPS * b), lambda i: (i, 0, 0))
    left = pl.pallas_call(
        slot_rows,
        grid=(slots // COUNT_GROUP,),
        out_shape=jax.ShapeDtypeStruct((slots, width, STEPS * b), BF16),
        in_specs=smem(1) + hbm(STEPS * NY),
        out_specs=left_part,
        scratch_shapes=[
            pltpu.VMEM((total_rows, STEPS, b, width), BF16),
            pltpu.SemaphoreType.DMA((STEPS * NY,)),
        ],
        compiler_params=room(9000),
        name="slot_rows",
    )(index, *forwards_0, *forwards_1)

    counts, beta_first, logs = pl.pallas_call(
        count_slots,
        grid=(slots // COUNT_GROUP,),
        out_shape=(
            jax.ShapeDtypeStruct((slots, width, width), BF16),
            jax.ShapeDtypeStruct((b, rows, width), F32),
            jax.ShapeDtypeStruct((STEPS, 128), F32),
        ),
        in_specs=smem(1) + hbm(STEPS + 1) + [left_part, part],
        out_specs=(
            part,
            pl.BlockSpec((b, rows, width), lambda i: (0, 0, 0)),
            pl.BlockSpec((STEPS, 128), lambda i: (0, 0)),
        ),
        scratch_shapes=[
            pltpu.VMEM((STEPS, total_cols, b, width), BF16),
            pltpu.VMEM((owners, lines + EXTRA, width), BF16),
            pltpu.VMEM((total_cols + 1, STEPS, b, width), BF16),
            pltpu.SemaphoreType.DMA((STEPS,)),
            pltpu.SemaphoreType.DMA,
        ],
        compiler_params=room(9000),
        name="count_slots",
    )(index, cols_0, cols_1, received_1, left, transitions)
    return counts, beta_first[:, :, None, :], logs[:, :b]


def solution(mesh):
    fine = Mesh(mesh.devices.reshape(NY, NH, NL, NX, NC), ALL)
    return jax.shard_map(
        steps,
        mesh=fine,
        in_specs=(
            P(ALL, None, None),
            P(ALL),
            P(ALL),
            P(None, DST, SRC, None),
            P(None, None, DST, SRC, None),
            P(None, None, DST, SRC, None),
        ),
        out_specs=(P(ALL, None, None), P(None, DST, SRC, None), P()),
        check_vma=False,
    )
```

```python
import functools

import jax
import jax.numpy as jnp
from jax import lax
from jax.experimental import pallas as pl
from jax.experimental.pallas import tpu as pltpu
from jax.sharding import Mesh
from jax.sharding import PartitionSpec as P


S = 131072
STEPS = 2
NY, NH, NL, NX, NC = 4, 4, 2, 4, 2
NZ = NH * NL
SRC_COUNT = NX * NC
DST = ("y", "zh", "zl")
NEAR = ("y", "zl")
NEAR_COUNT = NY * NL
SRC = ("x", "c")
ALL = DST + SRC
F32 = jnp.float32
BF16 = jnp.bfloat16
GRANT = 60 * 1024
EXTRA = 8
CHUNKS = 8
HELD = 12
COUNT_GROUP = 32
GROUP = 8


def room(kib):
    return pltpu.CompilerParams(vmem_limit_bytes=(GRANT - kib) * 1024)


def vmem(count):
    return [pl.BlockSpec(memory_space=pltpu.VMEM)] * count


def hbm(count):
    return [pl.BlockSpec(memory_space=pltpu.HBM)] * count


def smem(count):
    return [pl.BlockSpec(memory_space=pltpu.SMEM)] * count


def row_of(column, offset):
    b = column.shape[0]
    lane = lax.broadcasted_iota(jnp.int32, (b, 128), 1)
    seq = lax.broadcasted_iota(jnp.int32, (b, 128), 0)
    return jnp.sum(jnp.where(lane == seq + offset, column, 0.0), axis=0, keepdims=True)


def column_of(row, offset, b):
    lane = lax.broadcasted_iota(jnp.int32, (b, 128), 1)
    seq = lax.broadcasted_iota(jnp.int32, (b, 128), 0)
    wide = jnp.broadcast_to(row, (b, 128))
    return jnp.sum(jnp.where(lane == seq + offset, wide, 0.0), axis=1, keepdims=True)


def tree(values):
    while len(values) > 1:
        values = [values[n] + values[n + 1] for n in range(0, len(values), 2)]
    return values[0]


def over_slots(first, count, step):
    def several(g, carry):
        for n in range(GROUP):
            step(first + g * GROUP + n)
        return carry

    lax.fori_loop(0, count // GROUP, several, 0)


def load_blocks(blocks, held, sems):
    size = held.shape[0] // CHUNKS
    copies = []
    for n in range(CHUNKS):
        part = pl.ds(n * size, size)
        copies.append(pltpu.make_async_copy(blocks.at[part], held.at[part], sems.at[n]))
        copies[-1].start()
    return copies


def over_chunks(copies, held, step):
    size = held.shape[0] // CHUNKS
    for n, copy in enumerate(copies):
        copy.wait()
        over_slots(n * size, size, step)


def split_three(value, rows):
    high = value.astype(BF16).astype(F32)
    middle = (value - high).astype(BF16).astype(F32)
    low = value - high - middle
    line = lax.broadcasted_iota(jnp.int32, (rows, 128), 0)
    return jnp.where(
        line == 0, high, jnp.where(line == 1, middle, jnp.where(line == 2, low, 0.0))
    )


def multiply_slots(index, copies, held, cols, acc):
    acc[...] = jnp.zeros_like(acc)

    def step(m):
        product = lax.dot_general(
            cols[index[1, m]],
            held[m],
            (((1,), (1,)), ((), ())),
            preferred_element_type=F32,
        )
        row = index[0, m]
        acc[row] = acc[row] + product

    over_chunks(copies, held, step)


def send_partials(acc, ready, out, sems, extra=None):
    owners, lines = ready.shape[0], ready.shape[1]
    rows = acc.shape[0] // owners
    kept = rows * acc.shape[1]
    size = owners // CHUNKS
    copies = []
    for n in range(CHUNKS):
        part = pl.ds(n * size, size)
        value = acc[n * size * rows : (n + 1) * size * rows].astype(BF16)
        ready[part, :kept] = value.reshape(size, kept, 128)
        if extra is not None:
            ready[part, kept:] = jnp.broadcast_to(extra[None], (size, lines - kept, 128))
        copies.append(pltpu.make_async_copy(ready.at[part], out.at[part], sems.at[n]))
        copies[-1].start()
    return copies


def first_step(index, *refs):
    pieces, (blocks, out, cols_out) = refs[:SRC_COUNT], refs[SRC_COUNT : SRC_COUNT + 3]
    cols, acc, held, ready, in_sems, out_sems, col_sem = refs[SRC_COUNT + 3 :]
    copies = load_blocks(blocks, held, in_sems)
    rows = pieces[0].shape[0]
    for n, piece in enumerate(pieces):
        cols[n * rows : (n + 1) * rows] = piece[...]
    keep = pltpu.make_async_copy(cols, cols_out.at[pl.ds(0, cols.shape[0])], col_sem)
    keep.start()
    multiply_slots(index, copies, held, cols, acc)
    for copy in send_partials(acc, ready, out, out_sems):
        copy.wait()
    keep.wait()


def second_step(index, *refs):
    pieces, (blocks, out, cols_out) = refs[:SRC_COUNT], refs[SRC_COUNT : SRC_COUNT + 3]
    cols, acc, held, ready, in_sems, out_sems, col_sem = refs[SRC_COUNT + 3 :]
    copies = load_blocks(blocks, held, in_sems)
    b = acc.shape[1]
    rows = cols.shape[0] // SRC_COUNT
    parts = []
    for n, piece in enumerate(pieces):
        cols[n * rows : (n + 1) * rows] = piece[: rows * b].reshape(rows, b, 128)
        parts.append(norm_row(piece[rows * b :]))
    keep = pltpu.make_async_copy(cols, cols_out.at[pl.ds(0, cols.shape[0])], col_sem)
    keep.start()
    extra = split_three(tree(parts), EXTRA).astype(BF16)
    multiply_slots(index, copies, held, cols, acc)
    for copy in send_partials(acc, ready, out, out_sems, extra):
        copy.wait()
    keep.wait()


def back_products(index, *refs):
    forwards, (blocks, *outs) = refs[:NY], refs[NY : NY + 1 + NC]
    alphas, acc, held, in_sems, alpha_sems = refs[NY + 1 + NC :]
    per = forwards[0].shape[0]
    loads = []
    for n, alpha in enumerate(forwards):
        part = pl.ds(n * per, per)
        loads.append(pltpu.make_async_copy(alpha, alphas.at[part], alpha_sems.at[n]))
        loads[-1].start()
    copies = load_blocks(blocks, held, in_sems)
    acc[...] = jnp.zeros_like(acc)
    for load in loads:
        load.wait()

    def step(m):
        product = jnp.dot(alphas[index[2, m]], held[m], preferred_element_type=F32)
        col = index[3, m]
        acc[col] = acc[col] + product

    over_chunks(copies, held, step)
    rows = outs[0].shape[1]
    for k in range(NX):
        for h, out in enumerate(outs):
            first = (k * NC + h) * rows
            out[k] = acc[first : first + rows].astype(out.dtype)


def merge_cores(own, other, *outs):
    for k, out in enumerate(outs):
        out[...] = (own[k] + other[k].astype(F32)).astype(BF16)


def norm_row(lines):
    return jnp.sum(lines.astype(F32), axis=0, keepdims=True)


def hand_on(place, received, own, *pieces, kept):
    for k in range(NH):
        block = lax.bitwise_xor(place[0], k)
        total = received[0, block].astype(F32)
        for d in range(1, NEAR_COUNT):
            total = total + received[d, block].astype(F32)
        target = own if k == 0 else pieces[k - 1]
        target[:kept] = total[:kept].astype(target.dtype)
        if kept < total.shape[0]:
            norm = jnp.sum(total[kept:], axis=0, keepdims=True)
            target[kept:] = split_three(norm, EXTRA).astype(target.dtype)


def reduce_first(own, *refs):
    far, (emitted, alpha), backs = refs[: NH - 1], refs[NH - 1 : NH + 1], refs[NH + 1 : -1]
    message = refs[-1]
    rows, b = emitted.shape[0], emitted.shape[1]
    total = tree([own[...]] + [piece[...].astype(F32) for piece in far])
    total = total.reshape(rows, b, 128)
    sent = (emitted[...].astype(F32) * total).astype(BF16)
    message[: rows * b] = sent.reshape(rows * b, 128)
    back = tree([piece[...].astype(F32) for piece in backs])
    first = jnp.sum(total * alpha[...].astype(F32), axis=0)
    second = jnp.sum(sent.astype(F32) * back, axis=0)
    norm = row_of(jnp.sum(first, axis=1, keepdims=True), 0)
    norm = norm + row_of(jnp.sum(second, axis=1, keepdims=True), b)
    message[rows * b :] = split_three(norm, EXTRA).astype(BF16)


def slot_rows(index, *refs):
    forwards, (out, alphas, sems) = refs[: STEPS * NY], refs[STEPS * NY :]
    per = forwards[0].shape[0]

    @pl.when(pl.program_id(0) == 0)
    def _():
        copies = []
        for k in range(STEPS):
            for n in range(NY):
                at = NY * k + n
                target = alphas.at[pl.ds(n * per, per), k]
                copies.append(pltpu.make_async_copy(forwards[at], target, sems.at[at]))
                copies[-1].start()
        for copy in copies:
            copy.wait()

    step = pl.program_id(0)
    for n in range(out.shape[0]):
        m = step * out.shape[0] + n
        pair = [alphas[index[4, m], 0], alphas[index[2, m], 1]]
        out[n] = jnp.concatenate(pair, axis=0).T


def count_slots(index, *refs):
    messages, parts = refs[:STEPS], refs[STEPS : STEPS + NH]
    left, blocks, out, beta, logs, held, weighted, sems = refs[STEPS + NH :]
    b = weighted.shape[2]
    cols = held.shape[1]

    @pl.when(pl.program_id(0) == 0)
    def _():
        kept = parts[0].shape[0] - EXTRA
        copies = []
        for k in range(STEPS):
            kept_part = messages[k].at[pl.ds(0, cols)]
            copies.append(pltpu.make_async_copy(kept_part, held.at[k], sems.at[k]))
            copies[-1].start()
        norm = tree([norm_row(piece[kept:]) for piece in parts])
        total = tree([piece[:kept].astype(F32) for piece in parts])
        for copy in copies:
            copy.wait()
        weighted[cols] = jnp.zeros((STEPS, b, 128), BF16)
        for k in range(STEPS):
            inverse = S / column_of(norm, k * b, b)
            weighted[:cols, k] = (held[k].astype(F32) * inverse).astype(BF16)
        inverse = S / column_of(norm, b, b)
        for a in range(kept // b):
            beta[:, a, :] = total[a * b : (a + 1) * b] * inverse
        lane = lax.broadcasted_iota(jnp.int32, (1, 128), 1)
        first = jnp.where(lane < b, norm, 1.0)
        second = jnp.where((lane >= b) & (lane < 2 * b), norm, 1.0)
        moved = pltpu.roll(second, 128 - b, 1)
        logs[0:1, :] = jnp.log(first / S)
        logs[1:2, :] = jnp.log(moved / first)

    step = pl.program_id(0)
    for n in range(out.shape[0]):
        m = step * out.shape[0] + n
        right = weighted[index[3, m]].reshape(STEPS * b, 128)
        total = jnp.dot(left[n], right, preferred_element_type=F32)
        out[n] = (total * blocks[n].astype(F32)).astype(BF16)


def across(value, axis, size, k):
    return lax.ppermute(value, axis, [(i, i ^ k) for i in range(size)])


def gather_src(piece):
    found = [piece] + [across(piece, "x", NX, k) for k in range(1, NX)]
    out = []
    for item in found:
        out.append(item)
        out.append(across(item, "c", NC, 1))
    return out


def scatter(sent, place, lines, kept):
    received = lax.all_to_all(sent.reshape(NEAR_COUNT, NH, lines, 128), NEAR, 0, 0)
    own, *pieces = pl.pallas_call(
        functools.partial(hand_on, kept=kept),
        out_shape=(jax.ShapeDtypeStruct((lines, 128), F32),)
        + (jax.ShapeDtypeStruct((lines, 128), BF16),) * (NH - 1),
        in_specs=smem(1) + vmem(1),
        out_specs=tuple(vmem(NH)),
        compiler_params=room(9000),
    )(place, received)
    return [own] + [across(pieces[k - 1], "zh", NH, k) for k in range(1, NH)]


def gather_z(spread):
    column = lax.all_to_all(spread, ("zh", "zl"), 0, 0)
    return column.reshape((NZ * spread.shape[1],) + spread.shape[2:])


def gather_y(column):
    return [column] + [across(column, "y", NY, k) for k in range(1, NY)]


def steps(transitions, row_block, col_block, beta_last, emissions, forward):
    slots = transitions.shape[0]
    b, rows, width = beta_last.shape[0], beta_last.shape[1], beta_last.shape[3]
    owners = NY * NZ
    total_rows = rows * owners
    total_cols = rows * SRC_COUNT
    y = lax.axis_index("y")
    mine = lax.axis_index(SRC)

    living = row_block >= 0
    row_local = jnp.where(living, row_block // SRC_COUNT, 0)
    col_local = jnp.where(living, col_block % total_cols, 0)
    col_index = ((col_local % SRC_COUNT) ^ mine) * rows + col_local // SRC_COUNT
    per = total_rows // NY
    alpha_index = ((row_local // per) ^ y) * per + row_local % per
    owner = row_local // rows
    near = owner // NZ * NL + owner % NL
    placed = (near * NH + owner % NZ // NL) * rows + row_local % rows
    place = lax.axis_index("zh").astype(jnp.int32).reshape(1)
    index = jnp.stack(
        [
            jnp.where(living, placed, total_rows),
            col_index,
            alpha_index,
            jnp.where(living, col_index, total_cols),
            (owner ^ lax.axis_index(DST)) * rows + row_local % rows,
        ]
    )

    alpha = jnp.transpose(forward[:, :, :, 0, :], (0, 2, 1, 3))
    spread_1 = jnp.broadcast_to(alpha[1], (NZ,) + alpha.shape[1:])
    spread_1, emissions, beta_last = lax.optimization_barrier((spread_1, emissions, beta_last))
    emitted = jnp.transpose(emissions[:, :, :, 0, :], (0, 2, 1, 3))
    beta = jnp.transpose(beta_last[:, :, 0, :], (1, 0, 2))
    message = (emitted[0].astype(F32) * beta).astype(BF16)
    piece_shape = jax.ShapeDtypeStruct((rows, b, width), BF16)

    pieces = gather_src(message)

    forwards_1 = gather_y(gather_z(spread_1))
    pair = jnp.stack([alpha[0], across(alpha[0], "zl", NL, 1)])
    quads = [pair] + [across(pair, "zh", NH, k) for k in range(1, NH)]
    column = jnp.stack(quads).reshape(NZ * rows, b, width)
    forwards_0 = gather_y(column)

    def partial_shape(lines):
        return jax.ShapeDtypeStruct((owners, lines, width), BF16)

    def slot_scratch(lines):
        return [
            pltpu.VMEM((total_cols, b, width), BF16),
            pltpu.VMEM((total_rows + 8, b, width), F32),
            pltpu.VMEM((slots, width, width), BF16),
            pltpu.VMEM((owners, lines, width), BF16),
            pltpu.SemaphoreType.DMA((CHUNKS,)),
            pltpu.SemaphoreType.DMA((CHUNKS,)),
            pltpu.SemaphoreType.DMA,
        ]

    lines = rows * b
    cols_shape = jax.ShapeDtypeStruct((HELD * total_cols, b, width), BF16)

    sent, cols_0 = pl.pallas_call(
        first_step,
        out_shape=(partial_shape(lines), cols_shape),
        in_specs=smem(1) + vmem(SRC_COUNT) + hbm(1),
        out_specs=tuple(hbm(2)),
        scratch_shapes=slot_scratch(lines),
        compiler_params=room(9000),
        name="first_step",
    )(index, *pieces, transitions)
    received = scatter(sent, place, lines, lines)

    back_shape = (NX, rows, b, width)
    own_back, other_back = pl.pallas_call(
        back_products,
        out_shape=(
            jax.ShapeDtypeStruct(back_shape, F32),
            jax.ShapeDtypeStruct(back_shape, BF16),
        ),
        in_specs=smem(1) + hbm(NY + 1),
        out_specs=tuple(vmem(NC)),
        scratch_shapes=[
            pltpu.VMEM((total_rows, b, width), BF16),
            pltpu.VMEM((total_cols + 8, b, width), F32),
            pltpu.VMEM((slots, width, width), BF16),
            pltpu.SemaphoreType.DMA((CHUNKS,)),
            pltpu.SemaphoreType.DMA((NY,)),
        ],
        compiler_params=room(9000),
        name="back_products",
    )(index, *forwards_1, transitions)
    other_back = across(other_back, "c", NC, 1)
    backs = pl.pallas_call(
        merge_cores,
        out_shape=(piece_shape,) * NX,
        in_specs=vmem(2),
        out_specs=tuple(vmem(NX)),
        compiler_params=room(9000),
        name="merge_cores",
    )(own_back, other_back)
    backs = [backs[0]] + [across(backs[k], "x", NX, k) for k in range(1, NX)]

    message_1 = pl.pallas_call(
        reduce_first,
        out_shape=jax.ShapeDtypeStruct((lines + EXTRA, width), BF16),
        in_specs=vmem(NH + 2 + NX),
        out_specs=vmem(1)[0],
        compiler_params=room(9000),
        name="reduce_first",
    )(*received, emitted[1], alpha[0], *backs)
    pieces_1 = gather_src(message_1)

    sent_1, cols_1 = pl.pallas_call(
        second_step,
        out_shape=(partial_shape(lines + EXTRA), cols_shape),
        in_specs=smem(1) + vmem(SRC_COUNT) + hbm(1),
        out_specs=tuple(hbm(2)),
        scratch_shapes=slot_scratch(lines + EXTRA),
        compiler_params=room(9000),
        name="second_step",
    )(index, *pieces_1, transitions)
    received_1 = scatter(sent_1, place, lines + EXTRA, lines)

    part = pl.BlockSpec((COUNT_GROUP, width, width), lambda i: (i, 0, 0))
    left_part = pl.BlockSpec((COUNT_GROUP, width, STEPS * b), lambda i: (i, 0, 0))
    left = pl.pallas_call(
        slot_rows,
        grid=(slots // COUNT_GROUP,),
        out_shape=jax.ShapeDtypeStruct((slots, width, STEPS * b), BF16),
        in_specs=smem(1) + hbm(STEPS * NY),
        out_specs=left_part,
        scratch_shapes=[
            pltpu.VMEM((total_rows, STEPS, b, width), BF16),
            pltpu.SemaphoreType.DMA((STEPS * NY,)),
        ],
        compiler_params=room(9000),
        name="slot_rows",
    )(index, *forwards_0, *forwards_1)

    counts, beta_first, logs = pl.pallas_call(
        count_slots,
        grid=(slots // COUNT_GROUP,),
        out_shape=(
            jax.ShapeDtypeStruct((slots, width, width), BF16),
            jax.ShapeDtypeStruct((b, rows, width), F32),
            jax.ShapeDtypeStruct((STEPS, 128), F32),
        ),
        in_specs=smem(1) + hbm(STEPS) + vmem(NH) + [left_part, part],
        out_specs=(
            part,
            pl.BlockSpec((b, rows, width), lambda i: (0, 0, 0)),
            pl.BlockSpec((STEPS, 128), lambda i: (0, 0)),
        ),
        scratch_shapes=[
            pltpu.VMEM((STEPS, total_cols, b, width), BF16),
            pltpu.VMEM((total_cols + 1, STEPS, b, width), BF16),
            pltpu.SemaphoreType.DMA((STEPS,)),
        ],
        compiler_params=room(7600),
        name="count_slots",
    )(index, cols_0, cols_1, *received_1, left, transitions)
    return counts, beta_first[:, :, None, :], logs[:, :b]


def solution(mesh):
    fine = Mesh(mesh.devices.reshape(NY, NH, NL, NX, NC), ALL)
    return jax.shard_map(
        steps,
        mesh=fine,
        in_specs=(
            P(ALL, None, None),
            P(ALL),
            P(ALL),
            P(None, DST, SRC, None),
            P(None, None, DST, SRC, None),
            P(None, None, DST, SRC, None),
        ),
        out_specs=(P(ALL, None, None), P(None, DST, SRC, None), P()),
        check_vma=False,
    )
```
